32 devices in a mesh: dp: 16 (over z, x, core), head: 2 (over y).
Axes of the slice: x: 2, y: 2, z: 4, core: 2. Of those that a mesh axis runs over, the one named last changes fastest.
Arguments:
- tokens: bfloat16 [16, 1024, 768], P('dp'), may hold values from -6 to 6
- seg_ids: int32 [16, 1024], P('dp'), may hold values from 0 to 7, never falling along the last dimension, each value on 1 to 512 neighbouring positions
- row_fill: int32 [16], P('dp'), may hold values from 512 to 1024
- pos_table: bfloat16 [512, 768], P('dp'), may hold values from -6 to 6
- w_query: bfloat16 [768, 768], P(None, 'head'), may hold values from -0.21875 to 0.21875
- w_key: bfloat16 [768, 768], P(None, 'head'), may hold values from -0.21875 to 0.21875
- w_value: bfloat16 [768, 768], P(None, 'head'), may hold values from -0.21875 to 0.21875
- w_out: bfloat16 [768, 768], P('head'), may hold values from -0.875 to 0.875
- w_up: bfloat16 [768, 3072], P(None, 'head'), may hold values from -0.21875 to 0.21875
- w_down: bfloat16 [3072, 768], P('head'), may hold values from -0.109375 to 0.109375
- norm1_gain: float32 [768], replicated, may hold values from 0.25 to 1.75
- norm1_bias: float32 [768], replicated, may hold values from -3 to 3
- norm2_gain: float32 [768], replicated, may hold values from 0.25 to 1.75
- norm2_bias: float32 [768], replicated, may hold values from -3 to 3
- left_query: bfloat16 [768, 12], P('head'), may hold values from -1.75 to 1.75
- scale_query: float32 [12], replicated, may hold values from 0.25 to 1
- right_query: bfloat16 [12, 768], replicated, may hold values from -0.21875 to 0.21875
- left_key: bfloat16 [768, 12], P('head'), may hold values from -1.75 to 1.75
- scale_key: float32 [12], replicated, may hold values from 0.25 to 1
- right_key: bfloat16 [12, 768], replicated, may hold values from -0.21875 to 0.21875
- left_value: bfloat16 [768, 12], P('head'), may hold values from -1.75 to 1.75
- scale_value: float32 [12], replicated, may hold values from 0.25 to 1
- right_value: bfloat16 [12, 768], replicated, may hold values from -0.21875 to 0.21875
- left_out: bfloat16 [768, 12], replicated, may hold values from -6 to 6
- scale_out: float32 [12], replicated, may hold values from 0.25 to 1
- right_out: bfloat16 [12, 768], P(None, 'head'), may hold values from -0.875 to 0.875
- left_up: bfloat16 [3072, 12], P('head'), may hold values from -1.75 to 1.75
- scale_up: float32 [12], replicated, may hold values from 0.25 to 1
- right_up: bfloat16 [12, 768], replicated, may hold values from -0.21875 to 0.21875
- left_down: bfloat16 [768, 12], replicated, may hold values from -1.75 to 1.75
- scale_down: float32 [12], replicated, may hold values from 0.25 to 1
- right_down: bfloat16 [12, 3072], P(None, 'head'), may hold values from -0.109375 to 0.109375
- out_grad: bfloat16 [16, 1024, 768], P('dp'), may hold values from -6 to 6
Outputs:
- layer_out: bfloat16 [16, 1024, 768], P('dp')
- tokens_grad: float32 [16, 1024, 768], P('dp')
- grad_left_query: float32 [768, 12], P('head')
- grad_scale_query: float32 [12], replicated
- grad_right_query: float32 [12, 768], replicated
- grad_left_key: float32 [768, 12], P('head')
- grad_scale_key: float32 [12], replicated
- grad_right_key: float32 [12, 768], replicated
- grad_left_value: float32 [768, 12], P('head')
- grad_scale_value: float32 [12], replicated
- grad_right_value: float32 [12, 768], replicated
- grad_left_out: float32 [768, 12], replicated
- grad_scale_out: float32 [12], replicated
- grad_right_out: float32 [12, 768], P(None, 'head')
- grad_left_up: float32 [3072, 12], P('head')
- grad_scale_up: float32 [12], replicated
- grad_right_up: float32 [12, 768], replicated
- grad_left_down: float32 [768, 12], replicated
- grad_scale_down: float32 [12], replicated
- grad_right_down: float32 [12, 3072], P(None, 'head')
The draws below stay inside these ranges and needn't reach their ends.
All inputs are finite; a program needn't handle non-finite values.
Results may differ from the reference program's by a relative error of at most 0.033.
Values may be sent and summed in bfloat16 or wider, within the bound.
No kernel may reach another device: no remote copies, remote signals or barrier semaphores. Data moves between devices by JAX's collectives and lax.ppermute only.
A program may use at most 384 MiB of HBM per device.

```python
import math
import jax
import jax.numpy as jnp
import numpy as np
from jax import lax

D = 768
HEADS = 12
HEAD_DIM = 64
FF = 3072
SPAN = 256
RANK = 12
LEN = 1024
QBLK = 512
SEGS = 8
ROWS = 16
POS = 512


def touch_ends(array, key, smallest, largest):
    extent = array.shape
    index_at = [jax.random.randint(jax.random.fold_in(key, axis), (), 0, extent[axis]) for axis in range(len(extent))]
    array = array.at[tuple(index_at)].set(smallest)
    longest = extent.index(max(extent))
    index_at[longest] = (index_at[longest] + 1) % extent[longest]
    return array.at[tuple(index_at)].set(largest)


def level_of(rng, dims, shards, low, top_value):
    factor_of, own = 1.0, jax.random.fold_in(rng, 6)
    for position, blocks in shards:
        heights = jnp.exp(jax.random.uniform(jax.random.fold_in(own, position), (blocks,), jnp.float32, low / len(shards), top_value / len(shards)))
        factor_of = factor_of * jnp.repeat(heights, dims[position] // blocks).reshape([-1 if axis == position else 1 for axis in range(len(dims))])
    return factor_of


def profile(number_of, total, bound, lean):
    portions = [(1 << 20) // math.isqrt(standing ** lean) + 1 for standing in range(2, number_of + 1)]
    surplus, holding = total - bound - (number_of - 1), [1] * (number_of - 1)
    while surplus > 0:
        candidates = [i for i in range(number_of - 1) if holding[i] < bound]
        mass, remaining = sum([portions[i] for i in candidates]), surplus
        for i in candidates:
            addition = min(bound - holding[i], max(1, remaining * portions[i] // mass), surplus)
            holding[i] = holding[i] + addition
            surplus = surplus - addition
    return np.array([bound] + holding)


def ragged(rng, number_of, total, reach, skew):
    if number_of == 2:
        one = jax.random.randint(rng, (), max(1, total - reach), min(reach, total - 1) + 1)
        return jnp.stack([one, total - one])
    lengths = jnp.asarray(profile(number_of, total, reach, skew), jnp.int32)
    twos = (number_of - 1) // 2
    source_of, receiver = lengths[1:1 + 2 * twos:2], lengths[2:2 + 2 * twos:2]
    slack = jnp.minimum(source_of - 1, reach - receiver)
    passed = jax.random.randint(jax.random.fold_in(rng, 1), (twos,), 0, 1 << 20) % (slack + 1)
    lengths = lengths.at[1:1 + 2 * twos:2].set(source_of - passed).at[2:2 + 2 * twos:2].set(receiver + passed)
    return lengths[jax.random.permutation(jax.random.fold_in(rng, 2), number_of)]


def normal_values(key, shape, width, bound, shards=(), dtype=jnp.bfloat16):
    entries = width * jax.random.normal(key, shape, jnp.float32)
    if shards:
        entries = entries * level_of(key, shape, shards, -0.22, 0.18)
    return jnp.clip(entries, -bound, bound).astype(dtype)


def setup_inputs(seed: int = 0) -> dict:
    keys = jax.random.split(jax.random.key(seed), 34)
    return {
        "tokens": normal_values(keys[0], (ROWS, LEN, D), 1.0, 6.0, ((0, 16),)),
        "seg_ids": jax.vmap(lambda own: jnp.searchsorted(jnp.cumsum(ragged(own, SEGS, LEN, LEN // 2, 1)), jnp.arange(LEN), side="right"))(jax.random.split(keys[1], ROWS)).reshape((ROWS, LEN)).astype(jnp.int32),
        "row_fill": touch_ends(jax.random.randint(keys[2], (ROWS,), LEN // 2, LEN + 1), jax.random.fold_in(keys[2], 1), LEN // 2, LEN).astype(jnp.int32),
        "pos_table": normal_values(keys[3], (POS, D), 1.0, 6.0, ((0, 16),)),
        "w_query": normal_values(keys[4], (D, D), D ** -0.5, 0.21875, ((1, 2),)),
        "w_key": normal_values(keys[5], (D, D), D ** -0.5, 0.21875, ((1, 2),)),
        "w_value": normal_values(keys[6], (D, D), D ** -0.5, 0.21875, ((1, 2),)),
        "w_out": normal_values(keys[7], (D, D), (D // 16) ** -0.5, 0.875, ((0, 2),)),
        "w_up": normal_values(keys[8], (D, FF), D ** -0.5, 0.21875, ((1, 2),)),
        "w_down": normal_values(keys[9], (FF, D), FF ** -0.5, 0.109375, ((0, 2),)),
        "norm1_gain": jnp.clip(1.0 + 0.15 * jax.random.normal(keys[10], (D,), jnp.float32), 0.25, 1.75),
        "norm1_bias": normal_values(keys[11], (D,), 0.5, 3.0, (), jnp.float32),
        "norm2_gain": jnp.clip(1.0 + 0.15 * jax.random.normal(keys[12], (D,), jnp.float32), 0.25, 1.75),
        "norm2_bias": normal_values(keys[13], (D,), 0.5, 3.0, (), jnp.float32),
        "left_query": normal_values(keys[14], (D, RANK), RANK ** -0.5, 1.75, ((0, 2),)),
        "scale_query": jnp.clip(jnp.exp(jax.random.uniform(keys[15], (RANK,), jnp.float32, math.log(0.25), math.log(1.0))), 0.25, 1.0),
        "right_query": normal_values(keys[16], (RANK, D), D ** -0.5, 0.21875),
        "left_key": normal_values(keys[17], (D, RANK), RANK ** -0.5, 1.75, ((0, 2),)),
        "scale_key": jnp.clip(jnp.exp(jax.random.uniform(keys[18], (RANK,), jnp.float32, math.log(0.25), math.log(1.0))), 0.25, 1.0),
        "right_key": normal_values(keys[19], (RANK, D), D ** -0.5, 0.21875),
        "left_value": normal_values(keys[20], (D, RANK), RANK ** -0.5, 1.75, ((0, 2),)),
        "scale_value": jnp.clip(jnp.exp(jax.random.uniform(keys[21], (RANK,), jnp.float32, math.log(0.25), math.log(1.0))), 0.25, 1.0),
        "right_value": normal_values(keys[22], (RANK, D), D ** -0.5, 0.21875),
        "left_out": normal_values(keys[23], (D, RANK), 1.0, 6.0),
        "scale_out": jnp.clip(jnp.exp(jax.random.uniform(keys[24], (RANK,), jnp.float32, math.log(0.25), math.log(1.0))), 0.25, 1.0),
        "right_out": normal_values(keys[25], (RANK, D), (D // 16) ** -0.5, 0.875, ((1, 2),)),
        "left_up": normal_values(keys[26], (FF, RANK), RANK ** -0.5, 1.75, ((0, 2),)),
        "scale_up": jnp.clip(jnp.exp(jax.random.uniform(keys[27], (RANK,), jnp.float32, math.log(0.25), math.log(1.0))), 0.25, 1.0),
        "right_up": normal_values(keys[28], (RANK, D), D ** -0.5, 0.21875),
        "left_down": normal_values(keys[29], (D, RANK), RANK ** -0.5, 1.75),
        "scale_down": jnp.clip(jnp.exp(jax.random.uniform(keys[30], (RANK,), jnp.float32, math.log(0.25), math.log(1.0))), 0.25, 1.0),
        "right_down": normal_values(keys[31], (RANK, FF), FF ** -0.5, 0.109375, ((1, 2),)),
        "out_grad": normal_values(keys[32], (ROWS, LEN, D), 1.0, 6.0, ((0, 16),)),
    }


@jax.custom_vjp
def low(v):
    return lax.optimization_barrier(v.astype(jnp.bfloat16)).astype(jnp.float32)

@jax.custom_vjp
def low_back(v):
    return v

def low_keep(v):
    return (low(v), None)

def low_pass(kept, grad):
    return (grad,)

def back_keep(v):
    return (v, None)

def back_low(kept, grad):
    return (low(grad),)
low.defvjp(low_keep, low_pass)
low_back.defvjp(back_keep, back_low)
EPSILON = 1e-07

def matmul(left_mat, right_mat):
    return jnp.dot(left_mat, right_mat, precision=lax.Precision.HIGHEST)

def adapted(row_block, weight, triple):
    left_mat, scale_vec, right_mat = triple
    down_rows = matmul(row_block, right_mat.T)
    return matmul(row_block, weight) + matmul(down_rows * scale_vec, left_mat.T)

def normalize(hidden, norm_gain, norm_shift):
    row_mean = lax.optimization_barrier(jnp.mean(hidden, -1, keepdims=True))
    centred = hidden - row_mean
    variance = lax.optimization_barrier(jnp.mean(centred * centred, -1, keepdims=True))
    return centred * lax.rsqrt(variance + EPSILON) * norm_gain + norm_shift

def attention(query_row, key_row, value_row, seg_row, row_valid, pos_key, pos_query):
    factor = (3 * HEAD_DIM) ** (-0.5)
    query_heads = query_row.reshape(LEN, HEADS, HEAD_DIM)
    key_heads = key_row.reshape(LEN, HEADS, HEAD_DIM)
    value_heads = value_row.reshape(LEN, HEADS, HEAD_DIM)
    pos_key_heads = pos_key.reshape(2 * SPAN, HEADS, HEAD_DIM)
    pos_query_heads = pos_query.reshape(2 * SPAN, HEADS, HEAD_DIM)
    pos_to_key = low_back(jnp.einsum('khd,rhd->hkr', key_heads, pos_query_heads, precision=lax.Precision.HIGHEST))
    keys_pos = jnp.arange(LEN).astype(jnp.int32)

    def one_block(block_start):
        rows_pos = block_start + jnp.arange(QBLK).astype(jnp.int32)
        query_block = lax.dynamic_slice_in_dim(query_heads, block_start, QBLK, 0)
        seg_block = lax.dynamic_slice_in_dim(seg_row, block_start, QBLK, 0)
        content = jnp.einsum('bhd,khd->hbk', query_block, key_heads, precision=lax.Precision.HIGHEST)
        to_pos = low_back(jnp.einsum('bhd,rhd->hbr', query_block, pos_key_heads, precision=lax.Precision.HIGHEST))
        ahead_index = jnp.clip(rows_pos[:, None] - keys_pos[None, :], -SPAN, SPAN - 1) + SPAN
        behind = jnp.clip(keys_pos[:, None] - rows_pos[None, :], -SPAN, SPAN - 1) + SPAN
        picked = jnp.take_along_axis(to_pos, jnp.broadcast_to(ahead_index[None], (HEADS, QBLK, LEN)), axis=2)
        from_pos = jnp.take_along_axis(pos_to_key, jnp.broadcast_to(behind[None], (HEADS, LEN, QBLK)), axis=2).transpose(0, 2, 1)
        raw_sum = low_back(content + picked + from_pos) * factor
        allowed = (seg_block[:, None] == seg_row[None, :]) & (keys_pos < row_valid)[None, :] | (rows_pos[:, None] == keys_pos[None, :])
        scores = jnp.where(allowed[None], raw_sum, -jnp.inf)
        row_top = lax.optimization_barrier(jnp.max(scores, -1, keepdims=True))
        exp_scores = jnp.exp(scores - row_top)
        prob_block = exp_scores / lax.optimization_barrier(jnp.sum(exp_scores, -1, keepdims=True))
        return jnp.einsum('hbk,khd->bhd', low(prob_block), value_heads, precision=lax.Precision.HIGHEST)
    block_starts = (jnp.arange(LEN // QBLK) * QBLK).astype(jnp.int32)
    blocks = lax.map(jax.checkpoint(one_block), block_starts)
    return blocks.reshape(LEN, HEADS * HEAD_DIM)

def reference(tokens, seg_ids, row_fill, pos_table, w_query, w_key, w_value, w_out, w_up, w_down, norm1_gain, norm1_bias, norm2_gain, norm2_bias, left_query, scale_query, right_query, left_key, scale_key, right_key, left_value, scale_value, right_value, left_out, scale_out, right_out, left_up, scale_up, right_up, left_down, scale_down, right_down, out_grad):
    pos_rows = pos_table.astype(jnp.float32)
    query_w = w_query.astype(jnp.float32)
    key_w = w_key.astype(jnp.float32)
    value_w = w_value.astype(jnp.float32)
    out_w = w_out.astype(jnp.float32)
    up_w = w_up.astype(jnp.float32)
    down_w = w_down.astype(jnp.float32)
    adapters = tuple((matrix.astype(jnp.float32) for matrix in (left_query, scale_query, right_query, left_key, scale_key, right_key, left_value, scale_value, right_value, left_out, scale_out, right_out, left_up, scale_up, right_up, left_down, scale_down, right_down)))

    def forward(token_values, adapter_values):
        query_set = adapter_values[0:3]
        key_set = adapter_values[3:6]
        value_set = adapter_values[6:9]
        out_set = adapter_values[9:12]
        up_set = adapter_values[12:15]
        down_set = adapter_values[15:18]
        pos_query = low(adapted(pos_rows, query_w, query_set))
        pos_key = low(adapted(pos_rows, key_w, key_set))

        def one_row(scan_carry, scan_item):
            row_tokens, seg_row, row_valid = scan_item
            query_row = low_back(low(adapted(row_tokens, query_w, query_set)))
            key_row = low_back(low(adapted(row_tokens, key_w, key_set)))
            value_row = low_back(low(adapted(row_tokens, value_w, value_set)))
            attended = low_back(low(attention(query_row, key_row, value_row, seg_row, row_valid, pos_key, pos_query)))
            branch = low_back(adapted(attended, out_w, out_set))
            first_norm = normalize(row_tokens + branch, norm1_gain, norm1_bias)
            gate_in = low_back(adapted(low(first_norm), up_w, up_set))
            activated = low(jax.nn.gelu(gate_in, approximate=False))
            second = low_back(adapted(activated, down_w, down_set))
            return (scan_carry, normalize(first_norm + second, norm2_gain, norm2_bias))
        _, outputs = lax.scan(one_row, jnp.float32(0.0), (token_values, seg_ids, row_fill))
        return outputs
    outputs, pullback = jax.vjp(forward, tokens.astype(jnp.float32), adapters)
    tokens_grad, grads = pullback(out_grad.astype(jnp.float32))
    return (outputs.astype(jnp.bfloat16), tokens_grad, grads[0], grads[1], grads[2], grads[3], grads[4], grads[5], grads[6], grads[7], grads[8], grads[9], grads[10], grads[11], grads[12], grads[13], grads[14], grads[15], grads[16], grads[17])
```

```python
import math
from functools import partial

import jax
import jax.numpy as jnp
from jax import lax
from jax.experimental import pallas as pl
from jax.experimental.pallas import tpu as pltpu
from jax.sharding import PartitionSpec as P

HEAD_DIM = 64
EPSILON = 1e-07
RANKS = 16
TILE = 256
SPAN2 = 512
PAIR = 128
FACTOR = (3 * HEAD_DIM) ** (-0.5)
LOG2_SCALE = FACTOR * math.log2(math.e)
MASKED = -1e30
STEPS = (0, -1, 1, -2, 2)


def dot_nn(a, b):
    return lax.dot_general(a, b, (((1,), (0,)), ((), ())), preferred_element_type=jnp.float32)


def dot_nt(a, b):
    return lax.dot_general(a, b, (((1,), (1,)), ((), ())), preferred_element_type=jnp.float32)


def dot_tn(a, b):
    return lax.dot_general(a, b, (((0,), (0,)), ((), ())), preferred_element_type=jnp.float32)


def tile_iota(axis):
    return lax.broadcasted_iota(jnp.int32, (TILE, TILE), axis)


def lane_mask(half):
    lane = lax.broadcasted_iota(jnp.int32, (1, PAIR), 1)
    return (lane >= half * HEAD_DIM) & (lane < half * HEAD_DIM + HEAD_DIM)


def skew(table):
    return pltpu.roll(table, TILE + 1, 1, stride=1, stride_axis=0)


def unskew(flipped):
    return pltpu.roll(flipped, 0, 1, stride=1, stride_axis=0)


def shifted(table, rolled, step):
    if step == 0:
        return rolled[:, :TILE]
    top, bottom = table[:, SPAN2 - 1 :], table[:, :1]
    if step == -1:
        return jnp.where(tile_iota(1) <= tile_iota(0), rolled[:, TILE:], top)
    if step == 1:
        return jnp.where(tile_iota(1) > tile_iota(0), rolled[:, TILE:], bottom)
    return jnp.broadcast_to(top if step < 0 else bottom, (TILE, TILE))


def eye():
    return jnp.where(tile_iota(0) == tile_iota(1), 1.0, 0.0).astype(jnp.bfloat16)


def anti_eye():
    return jnp.where(tile_iota(0) + tile_iota(1) == TILE - 1, 1.0, 0.0).astype(jnp.bfloat16)


def block_rows(block):
    return pl.ds(pl.multiple_of(block * TILE, TILE), TILE)


def stacked(rows, masks):
    return jnp.concatenate([rows * mask for mask in masks], 0)


def doubled(lanes):
    return jnp.concatenate([lanes, lanes], 1)


def block_pairs(seg_ref, blocks, diagonal, neighbours, far):
    @pl.loop(0, blocks // 2)
    def _(i):
        diagonal(2 * i)
        diagonal(2 * i + 1)

    @pl.loop(0, blocks - 1)
    def _(i):
        neighbours(i, i + 1)

    @pl.loop(0, blocks - 2)
    def _(i):
        @pl.when(seg_ref[i * TILE + TILE - 1] == seg_ref[(i + 2) * TILE])
        def _():
            far(i, i + 2)


def forward_kernel(
    seg_ref, fill_ref, place_ref, q_ref, k_ref, v_ref, posq_ref, posk_ref, segk_ref,
    out_ref, send_ref, part_ref, inv_ref, column_ref, ahead_ref, ahead_edge, behind_ref, behind_edge, raw_ref, top_ref,
    acc_ref, summing_ref, posq_wide, posk_wide,
):
    blocks = q_ref.shape[0] // TILE
    masks = [jnp.where(lane_mask(half), 1.0, 0.0).astype(jnp.bfloat16) for half in range(2)]
    top_ref[...] = jnp.full_like(top_ref, MASKED)
    acc_ref[...] = jnp.zeros_like(acc_ref)
    for wide_ref, pos_ref in ((posq_wide, posq_ref), (posk_wide, posk_ref)):
        wide_ref[:SPAN2, :] = pos_ref[...]
        wide_ref[SPAN2 : SPAN2 + PAIR, :] = jnp.broadcast_to(pos_ref[:1, :], (PAIR, PAIR))
        wide_ref[SPAN2 + PAIR :, :] = jnp.broadcast_to(pos_ref[SPAN2 - 1 :, :], (PAIR, PAIR))

    @pl.loop(0, blocks)
    def _(block):
        rows = block_rows(block)
        column_ref[rows, :] = jnp.broadcast_to(
            segk_ref[block].astype(jnp.float32), (PAIR, TILE)
        ).T
        for half in range(2):
            summing_ref[half, rows, :] = jnp.where(lane_mask(half), v_ref[rows, :], 1.0).astype(
                jnp.bfloat16
            )
            table = dot_nt(k_ref[rows, :] * masks[half], posq_wide[...])
            behind_ref[half, rows, :] = skew(table[:, :SPAN2]).astype(jnp.bfloat16)
            behind_edge[half, rows, :] = table[:, SPAN2:].astype(jnp.bfloat16)
            table = dot_nt(q_ref[rows, :] * masks[half], posk_wide[...])
            ahead_ref[half, rows, :] = skew(table[:, :SPAN2])
            ahead_edge[half, rows, :] = table[:, SPAN2:]

    seye = eye()

    def biased(table_ref, edge_ref, half, rows, step):
        if step == 0:
            return table_ref[half, rows, :TILE]
        wide = doubled(edge_ref[half, rows, PAIR:] if step < 0 else edge_ref[half, rows, :PAIR])
        if abs(step) == 2:
            return wide
        if step == -1:
            keep = tile_iota(1) <= tile_iota(0)
        else:
            keep = tile_iota(1) > tile_iota(0)
        return jnp.where(keep, table_ref[half, rows, TILE:], wide)

    def score(block, key_block, step):
        qrows, rows = block_rows(block), block_rows(key_block)
        place_row = lax.broadcasted_iota(jnp.int32, (1, TILE), 1) + key_block * TILE
        allowed = doubled(column_ref[qrows, :]) == jnp.where(
            place_row < fill_ref[0], segk_ref[key_block].astype(jnp.float32), -1.0
        )
        if step == 0:
            allowed = allowed | (tile_iota(0) == tile_iota(1))
        for half in range(2):
            raw = (
                dot_nt(q_ref[qrows, :] * masks[half], k_ref[rows, :])
                + dot_nt(seye, biased(behind_ref, behind_edge, half, rows, -step))
                + biased(ahead_ref, ahead_edge, half, qrows, step)
            )
            raw = jnp.where(allowed, raw, MASKED)
            raw_ref[half, STEPS.index(step), qrows, :] = raw
            top_ref[half, qrows, :] = jnp.maximum(
                top_ref[half, qrows, :], jnp.max(raw, 1, keepdims=True)
            )

    def weigh(block, key_block, step):
        qrows, rows = block_rows(block), block_rows(key_block)
        place = STEPS.index(step)
        for half in range(2):
            part = jnp.exp2(
                (raw_ref[half, place, qrows, :] - doubled(top_ref[half, qrows, :])) * LOG2_SCALE
            )
            part_low = part.astype(jnp.bfloat16)
            part_ref[half, place, qrows, :] = part_low
            acc_ref[half, qrows, :] += dot_nn(part_low, summing_ref[half, rows, :])

    for body in (score, weigh):
        block_pairs(
            seg_ref, blocks,
            lambda block, body=body: body(block, block, 0),
            lambda first, second, body=body: (body(first, second, -1), body(second, first, 1)),
            lambda first, second, body=body: (body(first, second, -2), body(second, first, 2)),
        )

    @pl.loop(0, blocks)
    def _(block):
        qrows = block_rows(block)
        first, second = acc_ref[0, qrows, :], acc_ref[1, qrows, :]
        totals = pltpu.roll(jnp.where(lane_mask(0), second, first), HEAD_DIM, 1)
        inverse = 1.0 / totals
        inv_ref[qrows, :] = inverse
        out_ref[qrows, :] = (jnp.where(lane_mask(0), first, second) * inverse).astype(jnp.bfloat16)

    half_rows = send_ref.shape[0]
    send_ref[...] = out_ref[pl.ds(pl.multiple_of((1 - place_ref[0]) * half_rows, TILE), half_rows), :]


def backward_kernel(
    seg_ref, fill_ref, q_ref, k_ref, v_ref, posq_ref, posk_ref, att_ref, grad_ref, part_ref, inv_ref,
    dq_ref, dk_ref, dv_ref, dposq_ref, dposk_ref,
    dq_acc, dk_acc, dv_acc, diag_ref, row_high, key_high, row_clip, key_clip, dposq_acc, dposk_acc,
    grad_wide, value_wide, q_turned, g_turned,
):
    blocks = q_ref.shape[0] // TILE
    masks = [jnp.where(lane_mask(half), 1.0, 0.0).astype(jnp.bfloat16) for half in range(2)]
    flip = anti_eye()
    for ref in (dq_acc, dk_acc, dv_acc, row_high, key_high, row_clip, key_clip, dposq_acc, dposk_acc):
        ref[...] = jnp.zeros_like(ref)
    lane = lax.broadcasted_iota(jnp.int32, (TILE, PAIR), 1)

    def spread(folded, clips):
        turned = unskew(folded)
        return jnp.concatenate(
            [
                turned[:, :PAIR] + jnp.where(lane == 0, clips, 0.0),
                turned[:, PAIR : SPAN2 - PAIR],
                turned[:, SPAN2 - PAIR :] + jnp.where(lane == PAIR - 1, clips, 0.0),
            ],
            1,
        ).astype(jnp.bfloat16)

    @pl.loop(0, blocks)
    def _(block):
        qrows = block_rows(block)
        wide = grad_ref[qrows, :].astype(jnp.float32) * (inv_ref[qrows, :] * FACTOR)
        product = wide * att_ref[qrows, :].astype(jnp.float32)
        spot = lax.broadcasted_iota(jnp.int32, (TILE, PAIR), 1)
        for half in range(2):
            inner = jnp.sum(jnp.where(lane_mask(half), product, 0.0), 1, keepdims=True)
            high = inner.astype(jnp.bfloat16).astype(jnp.float32)
            free = (1 - half) * HEAD_DIM
            rest = jnp.where(spot == free, high, jnp.where(spot == free + 1, inner - high, 0.0))
            grad_wide[half, qrows, :] = jnp.where(lane_mask(half), wide, rest).astype(jnp.bfloat16)
            minus = jnp.where((spot == free) | (spot == free + 1), -1.0, 0.0)
            value_wide[half, qrows, :] = jnp.where(
                lane_mask(half), v_ref[qrows, :].astype(jnp.float32), minus
            ).astype(jnp.bfloat16)
        q_turned[block] = stacked(q_ref[qrows, :], masks).T
        g_turned[block] = stacked(wide.astype(jnp.bfloat16), masks).T

    def tile(block, key_block, step):
        qrows, rows = block_rows(block), block_rows(key_block)
        place = STEPS.index(step)
        below = tile_iota(1) <= tile_iota(0)
        under = tile_iota(1) < tile_iota(0)
        parts, grads = [], []
        for half in range(2):
            part_h = part_ref[half, place, qrows, :]
            dprob = dot_nt(grad_wide[half, qrows, :], value_wide[half, rows, :])
            wide = part_h.astype(jnp.float32) * dprob
            ds = wide.astype(jnp.bfloat16)
            parts.append(part_h)
            grads.append(ds)
            if step == 0:
                diag_ref[half, rows, :] = ds
            elif step == -1:
                row_high[half, qrows, :] = jnp.where(below, ds, row_high[half, qrows, :])
                key_high[half, rows, :] = jnp.where(under, ds, key_high[half, rows, :])
                row_clip[1, half, qrows, :] += jnp.sum(jnp.where(below, 0.0, wide), 1, keepdims=True)
                key_clip[half, key_block, 0:1] += jnp.sum(
                    jnp.where(under, 0.0, wide), 0, keepdims=True
                )
            elif step == 1:
                row_high[half, qrows, :] = jnp.where(below, row_high[half, qrows, :], ds)
                key_high[half, rows, :] = jnp.where(under, key_high[half, rows, :], ds)
                row_clip[0, half, qrows, :] += jnp.sum(jnp.where(below, wide, 0.0), 1, keepdims=True)
                key_clip[half, key_block, 1:2] += jnp.sum(
                    jnp.where(under, wide, 0.0), 0, keepdims=True
                )
            elif step == -2:
                row_clip[1, half, qrows, :] += jnp.sum(wide, 1, keepdims=True)
                key_clip[half, key_block, 0:1] += jnp.sum(wide, 0, keepdims=True)
            else:
                row_clip[0, half, qrows, :] += jnp.sum(wide, 1, keepdims=True)
                key_clip[half, key_block, 1:2] += jnp.sum(wide, 0, keepdims=True)
        dq_acc[qrows, :] += dot_nn(jnp.concatenate(grads, 1), stacked(k_ref[rows, :], masks))
        dv_acc[key_block] += dot_nn(g_turned[block], jnp.concatenate(parts, 0))
        dk_acc[key_block] += dot_nn(q_turned[block], jnp.concatenate(grads, 0))

    block_pairs(
        seg_ref, blocks,
        lambda block: tile(block, block, 0),
        lambda first, second: (tile(first, second, -1), tile(second, first, 1)),
        lambda first, second: (tile(first, second, -2), tile(second, first, 2)),
    )
    clip_row = lax.broadcasted_iota(jnp.int32, (PAIR, TILE), 0)

    @pl.loop(0, blocks)
    def _(block):
        rows = block_rows(block)
        q_spreads, k_spreads = [], []
        for half in range(2):
            clips = jnp.where(lane == 0, row_clip[0, half, rows, :], 0.0) + jnp.where(
                lane == PAIR - 1, row_clip[1, half, rows, :], 0.0
            )
            folded = dot_nn(
                flip,
                jnp.concatenate(
                    [diag_ref[half, rows, :], row_high[half, rows, :], clips.astype(jnp.bfloat16)], 1
                ),
            )
            q_spreads.append(spread(folded[:, :SPAN2], folded[:, SPAN2:]))
            clips = jnp.where(clip_row == 0, key_clip[half, block, 0:1], 0.0) + jnp.where(
                clip_row == PAIR - 1, key_clip[half, block, 1:2], 0.0
            )
            folded = dot_nt(
                flip,
                jnp.concatenate(
                    [diag_ref[half, rows, :], key_high[half, rows, :], clips.astype(jnp.bfloat16)], 0
                ),
            )
            k_spreads.append(spread(folded[:, :SPAN2], folded[:, SPAN2:]))
        flipped = dot_nn(
            flip, jnp.concatenate([q_ref[rows, :], k_ref[rows, :]], 1)
        ).astype(jnp.bfloat16)
        dposk_acc[...] += dot_tn(jnp.concatenate(q_spreads, 0), stacked(flipped[:, :PAIR], masks))
        dposq_acc[...] += dot_tn(jnp.concatenate(k_spreads, 0), stacked(flipped[:, PAIR:], masks))
        turned = jnp.concatenate(
            [
                dot_nn(jnp.concatenate(q_spreads, 1), stacked(posk_ref[...], masks)),
                dot_nn(jnp.concatenate(k_spreads, 1), stacked(posq_ref[...], masks)),
            ],
            1,
        ).astype(jnp.bfloat16)
        turned = dot_nn(flip, turned)
        dq_ref[rows, :] = (dq_acc[rows, :] + turned[:, :PAIR]).astype(jnp.bfloat16)
        dk_ref[rows, :] = (dk_acc[block].T + turned[:, PAIR:]).astype(jnp.bfloat16)
        dv_ref[rows, :] = (dv_acc[block].T * (1.0 / FACTOR)).astype(jnp.bfloat16)

    dposq_ref[...] = dposq_acc[...].astype(jnp.bfloat16)
    dposk_ref[...] = dposk_acc[...].astype(jnp.bfloat16)


def tile_facts(seg_row, row_valid):
    length = seg_row.shape[0]
    return seg_row, row_valid, seg_row.reshape(length // TILE, 1, TILE)


def pair_spec(rows):
    return pl.BlockSpec((rows, PAIR), lambda pair, *scalars: (0, pair))


def whole_spec(shape):
    return pl.BlockSpec(shape, lambda pair, *scalars: (0,) * len(shape))


def heads_spec(shape):
    return pl.BlockSpec((2,) + shape, lambda pair, *scalars: (pair,) + (0,) * len(shape))


def attend(place, query, key, value, posq, posk, facts):
    length, width = query.shape
    heads = width // HEAD_DIM
    seg, fill, segk = facts
    rows = pair_spec(length)
    pos = pair_spec(SPAN2)
    parts = (len(STEPS), length, TILE)
    return pl.pallas_call(
        forward_kernel,
        out_shape=(
            jax.ShapeDtypeStruct((length, width), jnp.bfloat16),
            jax.ShapeDtypeStruct((length // 2, width), jnp.bfloat16),
            jax.ShapeDtypeStruct((heads,) + parts, jnp.bfloat16),
            jax.ShapeDtypeStruct((length, width), jnp.float32),
        ),
        grid_spec=pltpu.PrefetchScalarGridSpec(
            num_scalar_prefetch=3,
            grid=(heads // 2,),
            in_specs=[rows, rows, rows, pos, pos, whole_spec(segk.shape)],
            out_specs=[rows, pair_spec(length // 2), heads_spec(parts), rows],
            scratch_shapes=[
                pltpu.VMEM((length, PAIR), jnp.float32),
                pltpu.VMEM((2, length, SPAN2), jnp.float32),
                pltpu.VMEM((2, length, 2 * PAIR), jnp.float32),
                pltpu.VMEM((2, length, SPAN2), jnp.bfloat16),
                pltpu.VMEM((2, length, 2 * PAIR), jnp.bfloat16),
                pltpu.VMEM((2,) + parts, jnp.float32),
                pltpu.VMEM((2, length, PAIR), jnp.float32),
                pltpu.VMEM((2, length, PAIR), jnp.float32),
                pltpu.VMEM((2, length, PAIR), jnp.bfloat16),
                pltpu.VMEM((SPAN2 + 2 * PAIR, PAIR), jnp.bfloat16),
                pltpu.VMEM((SPAN2 + 2 * PAIR, PAIR), jnp.bfloat16),
            ],
        ),
        name="attend",
        cost_estimate=pl.CostEstimate(
            flops=1_000_000_000, transcendentals=0, bytes_accessed=length * width,
        ),
    )(seg, fill, place, query, key, value, posq, posk, segk)


def attend_back(query, key, value, posq, posk, facts, attended, grad, part, inverse):
    length, width = query.shape
    heads = width // HEAD_DIM
    seg, fill = facts[:2]
    rows = pair_spec(length)
    pos = pair_spec(SPAN2)
    whole = jax.ShapeDtypeStruct((length, width), jnp.bfloat16)
    table = jax.ShapeDtypeStruct((SPAN2, width), jnp.bfloat16)
    parts = (len(STEPS), length, TILE)
    return pl.pallas_call(
        backward_kernel,
        out_shape=(whole, whole, whole, table, table),
        grid_spec=pltpu.PrefetchScalarGridSpec(
            num_scalar_prefetch=2,
            grid=(heads // 2,),
            in_specs=[rows, rows, rows, pos, pos, rows, rows, heads_spec(parts), rows],
            out_specs=[rows, rows, rows, pos, pos],
            scratch_shapes=[
                pltpu.VMEM((length, PAIR), jnp.float32),
                pltpu.VMEM((length // TILE, PAIR, TILE), jnp.float32),
                pltpu.VMEM((length // TILE, PAIR, TILE), jnp.float32),
                pltpu.VMEM((2, length, TILE), jnp.bfloat16),
                pltpu.VMEM((2, length, TILE), jnp.bfloat16),
                pltpu.VMEM((2, length, TILE), jnp.bfloat16),
                pltpu.VMEM((2, 2, length, 1), jnp.float32),
                pltpu.VMEM((2, length // TILE, 8, TILE), jnp.float32),
                pltpu.VMEM((SPAN2, PAIR), jnp.float32),
                pltpu.VMEM((SPAN2, PAIR), jnp.float32),
                pltpu.VMEM((2, length, PAIR), jnp.bfloat16),
                pltpu.VMEM((2, length, PAIR), jnp.bfloat16),
                pltpu.VMEM((length // TILE, PAIR, 2 * TILE), jnp.bfloat16),
                pltpu.VMEM((length // TILE, PAIR, 2 * TILE), jnp.bfloat16),
            ],
        ),
        name="attend_back",
        cost_estimate=pl.CostEstimate(
            flops=50_000_000_000, transcendentals=0, bytes_accessed=heads * length * TILE * 10
        ),
    )(seg, fill, query, key, value, posq, posk, attended, grad, part, inverse)


def normalize(hidden, norm_gain, norm_shift):
    row_mean = jnp.mean(hidden, -1, keepdims=True)
    centred = hidden - row_mean
    inverse = lax.rsqrt(jnp.mean(centred * centred, -1, keepdims=True) + EPSILON)
    normed = centred * inverse
    return (normed * norm_gain + norm_shift, normed, inverse)


def normalize_back(upstream, normed, inverse, norm_gain):
    scaled = upstream * norm_gain
    return inverse * (
        scaled
        - jnp.mean(scaled, -1, keepdims=True)
        - normed * jnp.mean(scaled * normed, -1, keepdims=True)
    )


def low(x):
    return x.astype(jnp.bfloat16)


def fetched_rows(width, hidden, local):
    pack = width + 2 * RANKS
    down = pack + hidden // 2
    return slice(0, pack), slice(pack, down), slice(down, down + local // 2)


def middle_kernel(
    place_ref, att_ref, other_ref, token_ref, grad_ref, out_own_ref, pack_own_ref, down_own_ref,
    got_ref, par_ref, norm_ref, right_out_ref, left_out_ref, right_up_ref, left_down_ref,
    layer_ref, first_grad_ref, heads_grad_ref, other_grad_ref, kept_ref, sent_ref,
    act_ref, slope_ref, left_up_acc, right_down_acc, left_out_acc, left_down_acc, right_up_acc,
    right_out_acc, right_other_acc, out_other_ref,
):
    width = token_ref.shape[1]
    local = att_ref.shape[1]
    chunks = []
    pack_rows, down_rows, out_rows = fetched_rows(width, down_own_ref.shape[0], local)
    right_other_ref = got_ref.at[out_rows.stop :, :local]
    for pack, down in (
        (pack_own_ref, down_own_ref),
        (got_ref.at[pack_rows], got_ref.at[down_rows]),
        (par_ref.at[pack_rows], par_ref.at[down_rows]),
    ):
        for start in range(0, down.shape[0], width):
            chunks.append((pack, down, slice(start, start + width)))
    gain1, shift1, gain2, shift2 = (norm_ref[i : i + 1, :] for i in range(4))
    accs = (left_up_acc, right_down_acc, left_out_acc, left_down_acc, right_up_acc,
            right_out_acc, right_other_acc)

    @pl.when(pl.program_id(0) == 0)
    def _():
        for acc in accs:
            acc[...] = jnp.zeros_like(acc)
        for core in range(2):

            @pl.when(place_ref[1] == core)
            def _():
                halves = (got_ref, par_ref) if core == 0 else (par_ref, got_ref)
                for index, ref in enumerate(halves):
                    out_other_ref[index * local // 2 : (index + 1) * local // 2, :] = ref[out_rows, :]

    att, other = att_ref[...], other_ref[...]
    branch = dot_nn(att, out_own_ref[...]) + dot_nn(other, out_other_ref[...])
    out_down = low(dot_nt(right_out_ref[...], att) + dot_nt(right_other_ref[...], other))
    first_norm, normed_first, inverse_first = normalize(
        token_ref[...].astype(jnp.float32) + branch, gain1, shift1
    )
    first_low = low(first_norm)
    up_down = low(dot_nt(right_up_ref[...], first_low))
    second_in = first_norm
    down_down = jnp.zeros((RANKS, token_ref.shape[0]), jnp.float32)
    for index, (pack, down, cols) in enumerate(chunks):
        gate = dot_nn(first_low, pack[:width, cols])
        cumulative = 0.5 + 0.5 * lax.erf(gate * (0.5**0.5))
        act = low(gate * cumulative)
        slope_ref[index] = cumulative + gate * (
            jnp.exp(-0.5 * gate * gate) * ((2.0 * math.pi) ** -0.5)
        )
        act_ref[index] = act
        second_in = second_in + dot_nn(act, down[cols, :])
        down_down = down_down + dot_nt(pack[width + RANKS :, cols], act)
    result, normed_second, inverse_second = normalize(second_in, gain2, shift2)
    layer_ref[...] = low(result)
    grad_second = normalize_back(
        grad_ref[...].astype(jnp.float32), normed_second, inverse_second, gain2
    )
    ffn_grad = low(grad_second)
    left_down_acc[...] += dot_nn(low(down_down), ffn_grad)
    down_back = low(dot_nt(left_down_ref[...], ffn_grad))
    grad_first = grad_second
    up_back = jnp.zeros((RANKS, token_ref.shape[0]), jnp.float32)
    for index, (pack, down, cols) in enumerate(chunks):
        gate_grad = low(dot_nt(ffn_grad, down[cols, :]) * slope_ref[index])
        grad_first = grad_first + dot_nt(gate_grad, pack[:width, cols])
        up_back = up_back + dot_nt(pack[width : width + RANKS, cols], gate_grad)
        left_up_acc[index] += dot_nn(up_down, gate_grad)
        right_down_acc[index] += dot_nn(down_back, act_ref[index])
    right_up_acc[...] += dot_nn(low(up_back), first_low)
    grad_first_in = normalize_back(grad_first, normed_first, inverse_first, gain1)
    first_grad_ref[...] = grad_first_in
    branch_grad = low(grad_first_in)
    heads_grad_ref[...] = low(dot_nt(branch_grad, out_own_ref[...]))
    other_grad_ref[...] = low(dot_nt(branch_grad, out_other_ref[...]))
    left_out_acc[...] += dot_nn(out_down, branch_grad)
    out_back = low(dot_nt(left_out_ref[...], branch_grad))
    right_out_acc[...] += dot_nn(out_back, att)
    right_other_acc[...] += dot_nn(out_back, other)

    @pl.when(pl.program_id(0) == pl.num_programs(0) - 1)
    def _():
        hidden = width * len(chunks) // 2
        scale_up = jnp.zeros((RANKS, 1), jnp.float32)
        for index, (pack, _, cols) in enumerate(chunks):
            scale_up = scale_up + jnp.sum(
                left_up_acc[index] * pack[width : width + RANKS, cols].astype(jnp.float32),
                1, keepdims=True,
            )
        scale_out = jnp.sum(left_out_acc[...] * left_out_ref[...].astype(jnp.float32), 1, keepdims=True)
        scale_down = jnp.sum(
            left_down_acc[...] * left_down_ref[...].astype(jnp.float32), 1, keepdims=True
        )
        lane = lax.broadcasted_iota(jnp.int32, (RANKS, PAIR), 1)
        scales = jnp.where(
            lane == 0, scale_up, jnp.where(lane == 1, scale_out, jnp.where(lane == 2, scale_down, 0.0))
        )
        base = 2 * hidden + local
        for ref in (kept_ref, sent_ref):
            ref[:, base : base + width] = low(left_out_acc[...])
            ref[:, base + width : base + 2 * width] = low(left_down_acc[...])
            ref[:, base + 2 * width : base + 3 * width] = low(right_up_acc[...])
            ref[:, base + 3 * width :] = low(scales)
        kept_ref[:, 2 * hidden : base] = low(right_out_acc[...])
        sent_ref[:, 2 * hidden : base] = low(right_other_acc[...])
        mine = len(chunks) // 2
        for index in range(mine):
            spot = slice(index * width, (index + 1) * width)
            kept_ref[:, spot] = low(left_up_acc[index])
            kept_ref[:, hidden + index * width : hidden + (index + 1) * width] = low(
                right_down_acc[index]
            )
        for core in range(2):

            @pl.when(place_ref[1] == core)
            def _():
                for index in range(mine):
                    source = mine + (index ^ core)
                    sent_ref[:, index * width : (index + 1) * width] = low(left_up_acc[source])
                    sent_ref[:, hidden + index * width : hidden + (index + 1) * width] = low(
                        right_down_acc[source]
                    )


def middle(place, attended, att_other, tokens, out_grad, out_own, pack_own, down_own, got, par, norms,
           right_out, left_out, right_up, left_down):
    length, width = tokens.shape
    local = attended.shape[1]
    hidden = pack_own.shape[1]
    half = length // 2
    tall = min(TILE, half)
    steps = half // tall
    chunks = 2 * hidden // width
    mine = lambda i, place: (place[0] * steps + i, 0)
    here = lambda i, place: (i, 0)
    whole = lambda a: pl.BlockSpec(a.shape, lambda i, place: (0,) * a.ndim)
    columns = 2 * hidden + local + 3 * width + PAIR
    consts = (out_own, pack_own, down_own, got, par, norms, right_out, left_out, right_up, left_down)
    bundle = jax.ShapeDtypeStruct((RANKS, columns), jnp.bfloat16)
    return pl.pallas_call(
        middle_kernel,
        out_shape=(
            jax.ShapeDtypeStruct((half, width), jnp.bfloat16),
            jax.ShapeDtypeStruct((half, width), jnp.float32),
            jax.ShapeDtypeStruct((length, local), jnp.bfloat16),
            jax.ShapeDtypeStruct((half, local), jnp.bfloat16),
            bundle,
            bundle,
        ),
        grid_spec=pltpu.PrefetchScalarGridSpec(
            num_scalar_prefetch=1,
            grid=(steps,),
            in_specs=[
                pl.BlockSpec((tall, local), mine), pl.BlockSpec((tall, local), here),
                pl.BlockSpec((tall, width), mine), pl.BlockSpec((tall, width), mine),
            ] + [whole(a) for a in consts],
            out_specs=[
                pl.BlockSpec((tall, width), here), pl.BlockSpec((tall, width), here),
                pl.BlockSpec((tall, local), mine), pl.BlockSpec((tall, local), here),
                whole(bundle), whole(bundle),
            ],
            scratch_shapes=[
                pltpu.VMEM((chunks, tall, width), jnp.bfloat16),
                pltpu.VMEM((chunks, tall, width), jnp.float32),
                pltpu.VMEM((chunks, RANKS, width), jnp.float32),
                pltpu.VMEM((chunks, RANKS, width), jnp.float32),
                pltpu.VMEM((RANKS, width), jnp.float32),
                pltpu.VMEM((RANKS, width), jnp.float32),
                pltpu.VMEM((RANKS, width), jnp.float32),
                pltpu.VMEM((RANKS, local), jnp.float32),
                pltpu.VMEM((RANKS, local), jnp.float32),
                pltpu.VMEM((local, width), jnp.bfloat16),
            ],
        ),
        name="middle",
        cost_estimate=pl.CostEstimate(
            flops=half * width * hidden * 20, transcendentals=half * hidden * 4,
            bytes_accessed=hidden * width * 8,
        ),
    )(place, attended, att_other, tokens, out_grad, *consts)


def input_grad_kernel(
    place_ref, dq_ref, dk_ref, dv_ref, wq_ref, wk_ref, wv_ref, spot_ref, after_ref, out_ref,
    *, first, steps,
):
    total = (
        dot_nt(dq_ref[...], wq_ref[...])
        + dot_nt(dk_ref[...], wk_ref[...])
        + dot_nt(dv_ref[...], wv_ref[...])
    )
    own = (pl.program_id(0) + first) // steps == place_ref[0]
    out_ref[...] = low(total + jnp.where(own, spot_ref[...], 0.0))


def input_grad(place, grads, weights, spot, start, count, after):
    local = grads[0].shape[1]
    half, width = spot.shape
    tall = min(TILE, count)
    steps, first = half // tall, start // tall
    rows = pl.BlockSpec((tall, local), lambda i, place: (i + first, 0))
    whole = pl.BlockSpec((width, local), lambda i, place: (0, 0))
    return pl.pallas_call(
        partial(input_grad_kernel, first=first, steps=steps),
        out_shape=jax.ShapeDtypeStruct((count, width), jnp.bfloat16),
        grid_spec=pltpu.PrefetchScalarGridSpec(
            num_scalar_prefetch=1,
            grid=(count // tall,),
            in_specs=[rows] * 3 + [whole] * 3 + [
                pl.BlockSpec(
                    (tall, width),
                    lambda i, place: (jnp.clip(i + first - place[0] * steps, 0, steps - 1), 0),
                ),
                pl.BlockSpec(memory_space=pl.ANY),
            ],
            out_specs=pl.BlockSpec((tall, width), lambda i, place: (i, 0)),
        ),
        name="input_grad",
        cost_estimate=pl.CostEstimate(
            flops=count * width * local * 6, transcendentals=0, bytes_accessed=8 * count * width
        ),
    )(place, *grads, *weights, spot, after)


def adapter_kernel(
    dq_ref, dk_ref, dv_ref, dposq_ref, dposk_ref, left_ref, token_down_ref, pos_down_ref, token_ref,
    pos_ref, kept_ref, got_ref, after_ref, out_ref,
):
    local = dq_ref.shape[1]
    width = token_ref.shape[1]
    lefts, backs = [], []
    for index, grad_ref in enumerate((dq_ref, dk_ref, dv_ref)):
        ranks = slice(index * RANKS, (index + 1) * RANKS)
        lefts.append(dot_nn(token_down_ref[ranks, :], grad_ref[...]))
        backs.append(low(dot_nt(left_ref[ranks, :], grad_ref[...])))
    pos_backs = []
    for index, grad_ref in enumerate((dposq_ref, dposk_ref)):
        ranks = slice(index * RANKS, (index + 1) * RANKS)
        lefts[index] = lefts[index] + dot_nn(pos_down_ref[ranks, :], grad_ref[...])
        pos_backs.append(low(dot_nt(left_ref[ranks, :], grad_ref[...])))
    rights = dot_nn(jnp.concatenate(backs, 0), token_ref[...])
    rights_pos = dot_nn(jnp.concatenate(pos_backs, 0), pos_ref[...])
    lane = lax.broadcasted_iota(jnp.int32, (RANKS, PAIR), 1)
    scales = jnp.zeros((RANKS, PAIR), jnp.float32)
    base = 3 * local
    for index in range(3):
        ranks = slice(index * RANKS, (index + 1) * RANKS)
        left = lefts[index]
        out_ref[:, index * local : (index + 1) * local] = low(left)
        scale = jnp.sum(left * left_ref[ranks, :].astype(jnp.float32), 1, keepdims=True)
        scales = jnp.where(lane == index, scale, scales)
        right = rights[ranks]
        if index < 2:
            right = right + rights_pos[ranks]
        out_ref[:, base + index * width : base + (index + 1) * width] = low(right)
    base = base + 3 * width
    out_ref[:, base : base + PAIR] = low(scales)
    out_ref[:, base + PAIR :] = low(
        kept_ref[...].astype(jnp.float32) + got_ref[...].astype(jnp.float32)
    )


def adapter_sums(grads, pos_grads, left, token_down, pos_down, tokens, pos_rows, kept, got, after):
    local, width = grads[0].shape[1], tokens.shape[1]
    columns = 3 * local + 3 * width + PAIR + kept.shape[1]
    args = (*grads, *pos_grads, left, token_down, pos_down, tokens, pos_rows, kept, got)
    return pl.pallas_call(
        adapter_kernel,
        out_shape=jax.ShapeDtypeStruct((RANKS, columns), jnp.bfloat16),
        in_specs=[pl.BlockSpec(memory_space=pltpu.VMEM)] * len(args)
        + [pl.BlockSpec(memory_space=pl.ANY)],
        out_specs=pl.BlockSpec(memory_space=pltpu.VMEM),
        name="adapter_sums",
        cost_estimate=pl.CostEstimate(
            flops=30_000_000_000, transcendentals=0, bytes_accessed=8 * tokens.size
        ),
    )(*args, after)


def pick_ranks(rank):
    rows = lax.broadcasted_iota(jnp.int32, (RANKS, rank), 0)
    return rows == lax.broadcasted_iota(jnp.int32, (RANKS, rank), 1)


def prepare_kernel(
    place_ref, wq_ref, wk_ref, wv_ref, wo_ref, wu_ref, wd_ref,
    lq_ref, sq_ref, rq_ref, lk_ref, sk_ref, rk_ref, lv_ref, sv_ref, rv_ref,
    lo_ref, so_ref, ro_ref, lu_ref, su_ref, ru_ref, ld_ref, sd_ref, rd_ref,
    mq_ref, mk_ref, mv_ref, mo_ref, pack_ref, md_ref,
    left_all_ref, right_all_ref, right_out_ref, left_out_ref, right_up_ref, left_down_ref,
    up_scaled_ref, down_scaled_ref, out_scaled_ref,
):
    rank = rq_ref.shape[0]
    width = wu_ref.shape[0]
    pick = pick_ranks(rank)
    pick_low = jnp.where(pick, 1.0, 0.0).astype(jnp.bfloat16)

    def padded(left_ref, scale_ref, right_ref):
        left = low(dot_nn(pick_low, left_ref[...]))
        right = low(dot_nn(pick_low, right_ref[...]))
        scale = jnp.sum(jnp.where(pick, scale_ref[...], 0.0), 1, keepdims=True)
        return left, right, low(right.astype(jnp.float32) * scale), scale

    def mixed(w_ref, left, scaled):
        return low(w_ref[...].astype(jnp.float32) + dot_tn(scaled, left))

    for index, (w_ref, out_ref, refs) in enumerate((
        (wq_ref, mq_ref, (lq_ref, sq_ref, rq_ref)),
        (wk_ref, mk_ref, (lk_ref, sk_ref, rk_ref)),
        (wv_ref, mv_ref, (lv_ref, sv_ref, rv_ref)),
    )):
        left, right, scaled, _ = padded(*refs)
        ranks = slice(index * RANKS, (index + 1) * RANKS)
        left_all_ref[ranks, :] = left
        right_all_ref[ranks, :] = right
        out_ref[...] = mixed(w_ref, left, scaled)
    left, right, scaled, scale = padded(lo_ref, so_ref, ro_ref)
    out_scaled_ref[...] = low(left.astype(jnp.float32) * scale)
    left_out_ref[...], right_out_ref[...] = left, right
    mo_ref[...] = mixed(wo_ref, left, scaled)
    left, right, scaled, _ = padded(lu_ref, su_ref, ru_ref)
    right_up_ref[...], up_scaled_ref[...] = right, scaled
    pack_ref[:width, :] = mixed(wu_ref, left, scaled)
    pack_ref[width : width + RANKS, :] = left
    left, right, scaled, scale = padded(ld_ref, sd_ref, rd_ref)
    down_scaled_ref[...] = low(left.astype(jnp.float32) * scale)
    left_down_ref[...] = left
    md_ref[...] = mixed(wd_ref, left, scaled)
    pack_ref[width + RANKS :, :] = right


def send_kernel(place_ref, wu_ref, wd_ref, wo_ref, lu_ref, rd_ref, ro_ref, send_ref):
    width, part = wu_ref.shape
    local = ro_ref.shape[1]
    pick = jnp.where(pick_ranks(lu_ref.shape[0]), 1.0, 0.0).astype(jnp.bfloat16)
    pack_rows, down_rows, out_rows = fetched_rows(width, 2 * part, local)
    send_ref[:width, :] = wu_ref[...]
    send_ref[width : width + RANKS, :] = low(dot_nn(pick, lu_ref[...]))
    send_ref[width + RANKS : width + 2 * RANKS, :] = low(dot_nn(pick, rd_ref[...]))
    send_ref[down_rows, :] = wd_ref[...]
    send_ref[out_rows, :] = wo_ref[...]
    send_ref[out_rows.stop :, :] = jnp.zeros((RANKS, width), jnp.bfloat16)
    send_ref[out_rows.stop :, :local] = low(dot_nn(pick, ro_ref[...]))


def weights_to_send(place, w_up, w_down, w_out, left_up, right_down, right_out):
    width, hidden = w_up.shape
    local, rank = w_out.shape[0], right_out.shape[0]
    part = hidden // 2
    rows = width + 3 * RANKS + part + local // 2
    by_lane = lambda tall: pl.BlockSpec((tall, part), lambda i, place: (0, place[1]))
    by_row = lambda tall: pl.BlockSpec((tall, width), lambda i, place: (place[1], 0))
    return pl.pallas_call(
        send_kernel,
        out_shape=jax.ShapeDtypeStruct((rows, width), jnp.bfloat16),
        grid_spec=pltpu.PrefetchScalarGridSpec(
            num_scalar_prefetch=1,
            grid=(1,),
            in_specs=[by_lane(width), by_row(part), by_row(local // 2), by_lane(rank), by_lane(rank),
                      pl.BlockSpec((rank, local), lambda i, place: (0, 0))],
            out_specs=pl.BlockSpec((rows, width), lambda i, place: (0, 0)),
        ),
        name="weights_to_send",
    )(place, w_up, w_down, w_out, left_up.T, right_down, right_out)


def fetched_kernel(place_ref, got_ref, up_ref, down_ref, out_ref, mixed_ref, *, other):
    width = up_ref.shape[1]
    part = got_ref.shape[1]
    local = 2 * (got_ref.shape[0] - width - 3 * RANKS - part)
    pack_rows, down_rows, out_rows = fetched_rows(width, 2 * part, local)
    left_up = got_ref[width : width + RANKS, :]
    right_down = got_ref[width + RANKS : width + 2 * RANKS, :]
    right_out = got_ref[out_rows.stop :, :local]
    mixed_ref[:width, :] = low(got_ref[:width, :].astype(jnp.float32) + dot_tn(up_ref[...], left_up))
    mixed_ref[width : width + 2 * RANKS, :] = got_ref[width : width + 2 * RANKS, :]
    mixed_ref[down_rows, :] = low(
        got_ref[down_rows, :].astype(jnp.float32) + dot_tn(right_down, down_ref[...])
    )
    term = dot_tn(right_out, out_ref[...])
    for core in range(2):

        @pl.when((place_ref[1] ^ other) == core)
        def _():
            mixed_ref[out_rows, :] = low(
                got_ref[out_rows, :].astype(jnp.float32)
                + term[core * local // 2 : (core + 1) * local // 2]
            )

    mixed_ref[out_rows.stop :, :] = got_ref[out_rows.stop :, :]


def fetched(place, got, up_scaled, down_scaled, out_scaled, other):
    vmem = pl.BlockSpec(memory_space=pltpu.VMEM)
    return pl.pallas_call(
        partial(fetched_kernel, other=other),
        out_shape=jax.ShapeDtypeStruct(got.shape, jnp.bfloat16),
        in_specs=[pl.BlockSpec(memory_space=pltpu.SMEM)] + [vmem] * 4,
        out_specs=vmem,
        name="fetched",
    )(place, got, up_scaled, down_scaled, out_scaled)


def prepare(place, weights, adapters):
    wq, wk, wv, wo, wu, wd = weights
    width, local = wq.shape
    hidden = wu.shape[1]
    args = list(weights)
    for left, scale, right in adapters:
        args += [left.T, scale.reshape(1, -1), right]
    bf16 = lambda *shape: jax.ShapeDtypeStruct(shape, jnp.bfloat16)
    vmem = pl.BlockSpec(memory_space=pltpu.VMEM)
    shapes = (
        bf16(width, local), bf16(width, local), bf16(width, local), bf16(local, width),
        bf16(width + 2 * RANKS, hidden), bf16(hidden, width),
        bf16(3 * RANKS, local), bf16(3 * RANKS, width), bf16(RANKS, local), bf16(RANKS, width),
        bf16(RANKS, width), bf16(RANKS, width),
        bf16(RANKS, width), bf16(RANKS, width), bf16(RANKS, width),
    )
    return pl.pallas_call(
        prepare_kernel,
        out_shape=shapes,
        in_specs=[pl.BlockSpec(memory_space=pltpu.SMEM)] + [vmem] * len(args),
        out_specs=[vmem] * len(shapes),
        name="prepare",
        cost_estimate=pl.CostEstimate(
            flops=40_000_000_000, transcendentals=0, bytes_accessed=8 * width * hidden
        ),
    )(place, *args)


def positions_kernel(
    index_ref, gathered_ref, wq_ref, wk_ref, right_ref, rows_ref, posq_ref, posk_ref, down_ref,
    *, shard, bits,
):
    count = gathered_ref.shape[0]
    spot = lax.broadcasted_iota(jnp.int32, (1, count), 1)
    owner = jnp.zeros((1, count), jnp.int32) + index_ref[0]
    for turn, bit in enumerate(bits):
        owner = owner ^ jnp.where((spot & (shard << turn)) != 0, bit, 0)
    origin = owner * shard + (spot & (shard - 1))
    wanted = count - 1 - lax.broadcasted_iota(jnp.int32, (count, 1), 0)
    turn = jnp.where(origin == wanted, 1.0, 0.0).astype(jnp.bfloat16)
    rows = low(dot_nn(turn, gathered_ref[...]))
    rows_ref[...] = rows
    posq_ref[...] = low(dot_nn(rows, wq_ref[...]))
    posk_ref[...] = low(dot_nn(rows, wk_ref[...]))
    down_ref[...] = low(dot_nt(right_ref[: 2 * RANKS, :], rows))


def positions(index, gathered, wq, wk, right_all, shard, bits):
    count, width = gathered.shape
    local = wq.shape[1]
    bf16 = lambda *shape: jax.ShapeDtypeStruct(shape, jnp.bfloat16)
    vmem = pl.BlockSpec(memory_space=pltpu.VMEM)
    return pl.pallas_call(
        partial(positions_kernel, shard=shard, bits=bits),
        out_shape=(bf16(count, width), bf16(count, local), bf16(count, local), bf16(2 * RANKS, count)),
        in_specs=[pl.BlockSpec(memory_space=pltpu.SMEM)] + [vmem] * 4,
        out_specs=[vmem] * 4,
        name="positions",
    )(index, gathered, wq, wk, right_all)


def swap_heads(x):
    return lax.ppermute(x, "head", [(0, 1), (1, 0)])


def swap_step(x, bit):
    count = lax.axis_size("dp")
    return lax.ppermute(x, "dp", [(i, i ^ bit) for i in range(count)])


def add_swapped(x, swapped):
    return x.astype(jnp.float32) + swapped.astype(jnp.float32)


def dp_bits():
    bits, bit = [1], 2
    while bit < lax.axis_size("dp"):
        bits = [bit] + bits
        bit *= 2
    return bits


def rows_of(x, start, count):
    return lax.dynamic_slice_in_dim(x, start, count, 0)


def gather_step(gathered, bit):
    return jnp.concatenate([gathered, swap_step(gathered, bit)], 0)


def shards(
    tokens, seg_ids, row_fill, pos_table,
    w_query, w_key, w_value, w_out, w_up, w_down,
    norm1_gain, norm1_bias, norm2_gain, norm2_bias,
    left_query, scale_query, right_query,
    left_key, scale_key, right_key,
    left_value, scale_value, right_value,
    left_out, scale_out, right_out,
    left_up, scale_up, right_up,
    left_down, scale_down, right_down,
    out_grad,
):
    length, width = tokens.shape[1:]
    local = w_query.shape[1]
    half = length // 2
    hidden = w_up.shape[1]
    rank = scale_query.shape[0]
    mine = lax.axis_index("head")
    core = lax.axis_index("dp") % 2
    my_start, other_start = mine * half, (1 - mine) * half
    token_rows = tokens[0]
    place = jnp.stack([mine, core]).astype(jnp.int32)

    bits = dp_bits()
    index = lax.axis_index("dp").reshape(1)
    gathered = gather_step(pos_table, bits[0])
    raw_send = weights_to_send(place, w_up, w_down, w_out, left_up, right_down, right_out)
    w_query, raw_send = lax.optimization_barrier((w_query, raw_send))
    weights_got = swap_heads(raw_send)
    (wq, wk, wv, out_own, pack_own, down_own, left_all, right_all,
     right_out_rows, left_out_rows, right_up_rows, left_down_rows,
     up_scaled, down_scaled, out_scaled) = prepare(
        place, (w_query, w_key, w_value, w_out, w_up, w_down),
        ((left_query, scale_query, right_query), (left_key, scale_key, right_key),
         (left_value, scale_value, right_value), (left_out, scale_out, right_out),
         (left_up, scale_up, right_up), (left_down, scale_down, right_down)),
    )
    gathered, wq = lax.optimization_barrier((gathered, wq))
    gathered = gather_step(gathered, bits[1])
    query = low(dot_nn(token_rows, wq))
    gathered, wk = lax.optimization_barrier((gathered, wk))
    for bit in bits[2:-1]:
        gathered = gather_step(gathered, bit)
    key = low(dot_nn(token_rows, wk))
    gathered, wv, right_all = lax.optimization_barrier((gathered, wv, right_all))
    gathered = gather_step(gathered, bits[-1])
    value = low(dot_nn(token_rows, wv))
    token_down = low(dot_nt(right_all, token_rows))
    pos_rows, posq, posk, pos_down = positions(
        index, gathered, wq, wk, right_all, pos_table.shape[0], bits
    )

    facts = tile_facts(seg_ids.reshape(length), row_fill)
    attended, att_send, probs, inverse = attend(place, query, key, value, posq, posk, facts)

    att_other = swap_heads(att_send)
    att_late, weights_got = lax.optimization_barrier((attended, weights_got))
    weights_par = swap_step(weights_got, 1)
    weights_got = fetched(place, weights_got, up_scaled, down_scaled, out_scaled, 0)
    weights_par = fetched(place, weights_par, up_scaled, down_scaled, out_scaled, 1)
    norms = jnp.concatenate(
        [jnp.stack([norm1_gain, norm1_bias, norm2_gain, norm2_bias]), jnp.zeros((4, width))], 0
    )
    layer_mine, grad_first_in, heads_grad, other_grad, kept, sent = middle(
        place, att_late, att_other, token_rows, out_grad[0],
        out_own, pack_own, down_own, weights_got, weights_par, norms,
        right_out_rows, left_out_rows, right_up_rows, left_down_rows,
    )
    heads_grad = lax.dynamic_update_slice_in_dim(heads_grad, swap_heads(other_grad), other_start, 0)
    kept_got = swap_heads(sent)
    layer_out = lax.dynamic_update_slice_in_dim(
        jnp.zeros((length, width), jnp.bfloat16), layer_mine, my_start, 0
    )
    layer_other = swap_heads(layer_mine)

    dq, dk, dv, dposq, dposk = attend_back(
        query, key, value, posq, posk, facts, attended, heads_grad, probs, inverse
    )
    dq, layer_other = lax.optimization_barrier((dq, layer_other))
    layer_out = lax.dynamic_update_slice_in_dim(layer_out, layer_other, other_start, 0)
    grads, weights = (dq, dk, dv), (wq, wk, wv)
    first, later = length // 4, 3 * length // 8
    first_sums = input_grad(place, grads, weights, grad_first_in, 0, first, dq)
    got_sums = [swap_heads(first_sums)]
    sums = adapter_sums(
        (dq, dk, dv), (dposq, dposk), left_all, token_down, pos_down, token_rows, pos_rows,
        kept, kept_got, first_sums,
    )
    split_at = 3 * local + 3 * width + PAIR
    cross = slice(3 * local, split_at)
    crossed = swap_heads(sums[:, cross])
    other_sums = input_grad(place, grads, weights, grad_first_in, first, 2 * later, sums)
    sent_sums = [first_sums, other_sums[:later], other_sums[later:]]
    crossed, got_sums[0], sent_sums[1] = lax.optimization_barrier(
        (crossed, got_sums[0], sent_sums[1])
    )
    got_sums.append(swap_heads(sent_sums[1]))
    sums = jnp.concatenate(
        [sums[:, : cross.start], low(add_swapped(sums[:, cross], crossed)), sums[:, cross.stop :]], 1
    )
    columns = sums.shape[1] // 2
    piece = lambda which: lax.dynamic_slice_in_dim(sums, which * columns, columns, 1)
    own = low(add_swapped(piece(core), swap_step(piece(1 - core), 1)))
    for turn, bit in enumerate(bits[:-1]):
        if turn == len(bits) - 2:
            own, got_sums[1] = lax.optimization_barrier((own, got_sums[1]))
            got_sums.append(swap_heads(sent_sums[2]))
        own = low(add_swapped(own, swap_step(own, bit)))
    other = swap_step(own, 1)
    sums = lax.dynamic_update_slice_in_dim(
        jnp.zeros((RANKS, 2 * columns), jnp.float32), own.astype(jnp.float32), core * columns, 1
    )
    sums = lax.dynamic_update_slice_in_dim(
        sums, other.astype(jnp.float32), (1 - core) * columns, 1
    )
    tokens_grad = jnp.concatenate([add_swapped(s, g) for s, g in zip(sent_sums, got_sums)], 0)
    late, early = sums[:, :split_at], sums[:, split_at:]
    def split(table, widths):
        pieces, start = [], 0
        for w in widths:
            pieces.append(table[:rank, start : start + w])
            start += w
        return pieces

    g_left_up, g_right_down, g_right_out, g_left_out, g_left_down, g_right_up, g_scales = split(
        early, [hidden, hidden, local, width, width, width, PAIR]
    )
    g_lq, g_lk, g_lv, g_rq, g_rk, g_rv, g_sqkv = split(
        late, [local, local, local, width, width, width, PAIR]
    )

    def left(table, scale):
        return (table * scale[:, None]).T

    def right(table, scale):
        return table * scale[:, None]

    return (
        layer_out[None],
        tokens_grad[None],
        left(g_lq, scale_query), g_sqkv[:, 0], right(g_rq, scale_query),
        left(g_lk, scale_key), g_sqkv[:, 1], right(g_rk, scale_key),
        left(g_lv, scale_value), g_sqkv[:, 2], right(g_rv, scale_value),
        left(g_left_out, scale_out), g_scales[:, 1], right(g_right_out, scale_out),
        left(g_left_up, scale_up), g_scales[:, 0], right(g_right_up, scale_up),
        left(g_left_down, scale_down), g_scales[:, 2], right(g_right_down, scale_down),
    )


def solution(mesh):
    in_specs = (
        P("dp", None, None),
        P("dp", None),
        P("dp"),
        P("dp", None),
        P(None, "head"),
        P(None, "head"),
        P(None, "head"),
        P("head", None),
        P(None, "head"),
        P("head", None),
        P(),
        P(),
        P(),
        P(),
        P("head", None),
        P(),
        P(),
        P("head", None),
        P(),
        P(),
        P("head", None),
        P(),
        P(),
        P(),
        P(),
        P(None, "head"),
        P("head", None),
        P(),
        P(),
        P(),
        P(),
        P(None, "head"),
        P("dp", None, None),
    )
    out_specs = (
        P("dp", None, None),
        P("dp", None, None),
        P("head", None),
        P(),
        P(),
        P("head", None),
        P(),
        P(),
        P("head", None),
        P(),
        P(),
        P(),
        P(),
        P(None, "head"),
        P("head", None),
        P(),
        P(),
        P(),
        P(),
        P(None, "head"),
    )
    return jax.shard_map(shards, mesh=mesh, in_specs=in_specs, out_specs=out_specs, check_vma=False)
```
